32 devices in a mesh: replica: 8 (over z, x), shard: 4 (over y, core).
Axes of the slice: x: 2, y: 2, z: 4, core: 2. Of those that a mesh axis runs over, the one named last changes fastest.
Arguments:
- hidden_in: bfloat16 [4096, 768], P(('replica', 'shard')), may hold values from -6 to 6
- out_cot: bfloat16 [4096, 768], P(('replica', 'shard')), may hold values from -6 to 6
- pre_gain: float32 [2, 768], replicated, may hold values from 0.5 to 1.5
- in_weight: bfloat16 [2, 768, 3352], P(None, 'shard'), may hold values from -0.21875 to 0.21875
- conv_weight: float32 [2, 4, 1792], replicated, may hold values from -2.4 to 2.4
- conv_bias: float32 [2, 1792], replicated, may hold values from -0.5 to 0.5
- dt_bias: float32 [2, 24], replicated, may hold values from -6 to -2
- a_log: float32 [2, 24], replicated, may hold values from -1.2 to 2
- skip: float32 [2, 24], replicated, may hold values from 0.5 to 1.5
- norm_gain: float32 [2, 1536], replicated, may hold values from 0.5 to 1.5
- out_weight: bfloat16 [2, 1536, 768], P(None, 'shard'), may hold values from -0.15625 to 0.15625
Outputs:
- block_out: bfloat16 [4096, 768], P(('replica', 'shard'))
- grad_in: float32 [4096, 768], P(('replica', 'shard'))
- grad_pre_gain: float32 [2, 768], replicated
- grad_in_weight: float32 [2, 768, 3352], P(None, 'shard')
- grad_conv_weight: float32 [2, 4, 1792], replicated
- grad_conv_bias: float32 [2, 1792], replicated
- grad_dt_bias: float32 [2, 24], replicated
- grad_a_log: float32 [2, 24], replicated
- grad_skip: float32 [2, 24], replicated
- grad_norm_gain: float32 [2, 1536], replicated
- grad_out_weight: float32 [2, 1536, 768], P(None, 'shard')
The draws below stay inside these ranges and needn't reach their ends.
All inputs are finite; a program needn't handle non-finite values.
Results may differ from the reference program's by a relative error of at most 0.014.
Values may be sent and summed in bfloat16 or wider, within the bound.
A program may use at most 192 MiB of HBM per device.

```python
import jax
import jax.numpy as jnp
from jax import lax

D = 768
DI = 1536
HEADS = 24
HEAD_DIM = 64
STATE = 128
CONV = 4
SPAN = 128
LAYERS = 2
TOK_DEV = 128
SEQ_LEN = 512
SEQS = 8
ROWS = 4096
PROJ = 3352
CHANNELS = 1792
N_SHARD = 4


def block_scale(stream_key, dims, shards, smallest, top_value):
    level = 1.0
    for axis_at, shards_of in shards:
        draws = jax.random.uniform(jax.random.fold_in(jax.random.fold_in(stream_key, 6), axis_at), (shards_of,), jnp.float32, smallest / len(shards), top_value / len(shards))
        level = level * jnp.repeat(jnp.exp(draws), dims[axis_at] // shards_of).reshape((-1,) + (1,) * (len(dims) - 1 - axis_at))
    return level


def scatter_about(stream_key, shape, deviation, limit, cuts=(), dtype=jnp.bfloat16):
    level = block_scale(stream_key, shape, cuts, -0.22, 0.18) if cuts else 1.0
    entries = jax.random.normal(stream_key, shape, jnp.float32) * deviation * level
    return jnp.minimum(jnp.maximum(entries, -limit), limit).astype(dtype)


def setup_inputs(seed: int = 0) -> dict:
    key_list = jax.random.split(jax.random.key(seed), 12)
    hidden_in = scatter_about(key_list[0], (ROWS, D), 1.0, 6.0, ((0, 32),))
    out_cot = scatter_about(key_list[1], (ROWS, D), 1.0, 6.0, ((0, 32),))
    pre_gain = jnp.clip(1.0 + 0.1 * jax.random.normal(key_list[2], (LAYERS, D), jnp.float32), 0.5, 1.5)
    in_weight = scatter_about(key_list[3], (LAYERS, D, PROJ), D ** -0.5, 0.21875, ((1, 4),))
    conv_weight = scatter_about(key_list[4], (LAYERS, CONV, CHANNELS), 0.4, 2.4, (), jnp.float32)
    conv_bias = jnp.clip(jax.random.uniform(key_list[5], (LAYERS, CHANNELS), jnp.float32, -0.5, 0.5), -0.5, 0.5)
    dt_bias = jnp.clip(jax.random.uniform(key_list[6], (LAYERS, HEADS), jnp.float32, -6.0, -2.0), -6.0, -2.0)
    a_log = jnp.clip(jax.random.uniform(key_list[7], (LAYERS, HEADS), jnp.float32, -1.2, 2.0), -1.2, 2.0)
    skip = jnp.clip(jax.random.uniform(key_list[8], (LAYERS, HEADS), jnp.float32, 0.5, 1.5), 0.5, 1.5)
    norm_gain = jnp.clip(1.0 + 0.1 * jax.random.normal(key_list[9], (LAYERS, DI), jnp.float32), 0.5, 1.5)
    out_weight = scatter_about(key_list[10], (LAYERS, DI, D), DI ** -0.5, 0.15625, ((1, 4),))
    return {"hidden_in": hidden_in, "out_cot": out_cot, "pre_gain": pre_gain, "in_weight": in_weight, "conv_weight": conv_weight, "conv_bias": conv_bias, "dt_bias": dt_bias, "a_log": a_log, "skip": skip, "norm_gain": norm_gain, "out_weight": out_weight}


EPS = 1e-05
EXACT = lax.Precision.HIGHEST

def rms_scale(residual, gain):
    mean_sq = lax.optimization_barrier(jnp.mean(residual * residual, axis=-1, keepdims=True))
    return residual * lax.rsqrt(mean_sq + EPS) * gain

def compose(earlier, later):
    return (earlier[0] * later[0], later[1] + later[0][..., None, None] * earlier[1])

def unpack(projected, rim_rows):
    channels = DI + 2 * STATE
    xbc_ext = jnp.concatenate([rim_rows, projected[:, DI:DI + channels]], axis=0).astype(jnp.float32)
    return (xbc_ext, projected[:, DI + channels:].astype(jnp.float32), projected[:, :DI].astype(jnp.float32))

def prepare(xbc_ext, dt_raw, conv_w, conv_b, dt_shift, a_log):
    length = xbc_ext.shape[0] - (CONV - 1)
    conv_out = conv_b + conv_w[0] * xbc_ext[0:length]
    for offset in range(1, CONV):
        conv_out = conv_out + conv_w[offset] * xbc_ext[offset:offset + length]
    activated = jax.nn.silu(conv_out)
    blocks = length // SPAN
    x_heads = activated[:, :DI].reshape(blocks, SPAN, HEADS, HEAD_DIM)
    write_proj = activated[:, DI:DI + STATE].reshape(blocks, SPAN, STATE)
    read_proj = activated[:, DI + STATE:].reshape(blocks, SPAN, STATE)
    step_size = jax.nn.softplus(dt_raw + dt_shift)
    decay_rate = -jnp.exp(a_log)
    log_decay = jnp.cumsum((step_size * decay_rate).reshape(blocks, SPAN, HEADS), axis=1)
    return (x_heads, write_proj, read_proj, step_size.reshape(blocks, SPAN, HEADS), log_decay)

def states(x_heads, write_proj, step_size, log_decay):
    to_end = jnp.exp(log_decay[:, -1:, :] - log_decay) * step_size
    weighted = x_heads * to_end[..., None]
    span_sum = jnp.einsum('cshp,csn->chpn', weighted, write_proj, precision=EXACT)
    span_decay = jnp.exp(log_decay[:, -1, :])

    def fold(carry, item):
        return (compose(carry, item), None)
    begin = (jnp.ones_like(span_decay[0]), jnp.zeros_like(span_sum[0]))
    total, _ = lax.scan(fold, begin, (span_decay, span_sum))
    return (total[1], total[0], span_sum, span_decay)

def outputs(x_heads, write_proj, read_proj, step_size, log_decay, span_sum, span_decay, entering, zgate, skip_gain, norm_gain):

    def advance(carry, item):
        return (item[1] + item[0][:, None, None] * carry, carry)
    _, before = lax.scan(advance, entering, (span_decay, span_sum))
    scores = jnp.einsum('ctn,csn->cts', read_proj, write_proj, precision=EXACT)
    decay_heads = jnp.swapaxes(log_decay, 1, 2)
    step_heads = jnp.swapaxes(step_size, 1, 2)
    gap = decay_heads[:, :, :, None] - decay_heads[:, :, None, :]
    causal = (jnp.arange(SPAN)[:, None] >= jnp.arange(SPAN)[None, :])[None, None, :, :]
    mixing = jnp.exp(jnp.where(causal, gap, -jnp.inf)) * scores[:, None, :, :] * step_heads[:, :, None, :]
    inside = jnp.einsum('chts,cshp->cthp', mixing, x_heads, precision=EXACT)
    carried = jnp.einsum('ctn,chpn->cthp', read_proj, before, precision=EXACT) * jnp.exp(log_decay)[..., None]
    mixed = inside + carried + skip_gain[:, None] * x_heads
    flat_rows = mixed.reshape(-1, HEADS * HEAD_DIM)
    return rms_scale(flat_rows * jax.nn.silu(zgate), norm_gain)

def inner_rows(left, right):
    return lax.dot_general(left, right, (((0,), (0,)), ((), ())), preferred_element_type=jnp.float32)

def outer_cols(left, right):
    return lax.dot_general(left, right, (((1,), (1,)), ((), ())), preferred_element_type=jnp.float32)

def reference(hidden_in, out_cot, pre_gain, in_weight, conv_weight, conv_bias, dt_bias, a_log, skip, norm_gain, out_weight):
    rim_width = CONV - 1
    channels = DI + 2 * STATE

    def one_sequence(totals, pair):
        seq_in, seq_cot = pair
        residual = seq_in.astype(jnp.float32)
        saved = []
        for section_no in range(LAYERS):
            normed = rms_scale(residual, pre_gain[section_no]).astype(jnp.bfloat16)
            projected = jnp.dot(normed, in_weight[section_no], preferred_element_type=jnp.float32).astype(jnp.bfloat16)
            carry_state = jnp.zeros((HEADS, HEAD_DIM, STATE), jnp.float32)
            rims = []
            enters = []
            parts = []
            for segment in range(N_SHARD):
                lower = segment * TOK_DEV
                if segment == 0:
                    rim_rows = jnp.zeros((rim_width, channels), jnp.bfloat16)
                else:
                    rim_rows = projected[lower - rim_width:lower, DI:DI + channels]
                xbc_ext, dt_raw, zgate = unpack(projected[lower:lower + TOK_DEV], rim_rows)
                pieces = prepare(xbc_ext, dt_raw, conv_weight[section_no], conv_bias[section_no], dt_bias[section_no], a_log[section_no])
                st_tot, dec_tot, span_sum, span_decay = states(pieces[0], pieces[1], pieces[3], pieces[4])
                parts.append(outputs(pieces[0], pieces[1], pieces[2], pieces[3], pieces[4], span_sum, span_decay, carry_state, zgate, skip[section_no], norm_gain[section_no]))
                rims.append(rim_rows)
                enters.append(carry_state)
                carry_state = st_tot + dec_tot[:, None, None] * carry_state
            gated_out = jnp.concatenate(parts, axis=0).astype(jnp.bfloat16)
            saved.append((residual, normed, projected, rims, enters, gated_out))
            residual = residual + jnp.dot(gated_out, out_weight[section_no], preferred_element_type=jnp.float32)
        block_out = residual.astype(jnp.bfloat16)
        cotangent = seq_cot.astype(jnp.float32)
        grads = [None] * LAYERS
        for section_no in reversed(range(LAYERS)):
            residual_in, normed, projected, rims, enters, gated_out = saved[section_no]
            cot_bf = cotangent.astype(jnp.bfloat16)
            grad_out_w = inner_rows(gated_out, cot_bf)
            grad_gated = outer_cols(cot_bf, out_weight[section_no])
            records = []
            for segment in range(N_SHARD):
                lower = segment * TOK_DEV
                xbc_ext, dt_raw, zgate = unpack(projected[lower:lower + TOK_DEV], rims[segment])
                pieces, prep_back = jax.vjp(prepare, xbc_ext, dt_raw, conv_weight[section_no], conv_bias[section_no], dt_bias[section_no], a_log[section_no])
                stats, state_back = jax.vjp(states, pieces[0], pieces[1], pieces[3], pieces[4])
                _, out_back = jax.vjp(outputs, pieces[0], pieces[1], pieces[2], pieces[3], pieces[4], stats[2], stats[3], enters[segment], zgate, skip[section_no], norm_gain[section_no])
                records.append((prep_back, state_back, stats[1], out_back(grad_gated[lower:lower + TOK_DEV])))
            later_grad = jnp.zeros((HEADS, HEAD_DIM, STATE), jnp.float32)
            laters = [None] * N_SHARD
            for segment in reversed(range(N_SHARD)):
                laters[segment] = later_grad
                later_grad = records[segment][3][7] + records[segment][2][:, None, None] * later_grad
            exts = []
            row_parts = []
            small_acc = None
            for segment in range(N_SHARD):
                prep_back, state_back, dec_tot, back_out = records[segment]
                later = laters[segment]
                grad_dec = lax.optimization_barrier(jnp.sum(later * enters[segment], axis=(1, 2)))
                from_state = state_back((later, grad_dec, back_out[5], back_out[6]))
                from_prep = prep_back((back_out[0] + from_state[0], back_out[1] + from_state[1], back_out[2], back_out[3] + from_state[2], back_out[4] + from_state[3]))
                exts.append(from_prep)
                fresh = (from_prep[2], from_prep[3], from_prep[4], from_prep[5], back_out[9], back_out[10])
                if small_acc is None:
                    small_acc = fresh
                else:
                    small_acc = tuple((old + new for old, new in zip(small_acc, fresh)))
            for segment in range(N_SHARD):
                own = exts[segment][0][rim_width:]
                if segment + 1 < N_SHARD:
                    own = own.at[TOK_DEV - rim_width:].add(exts[segment + 1][0][:rim_width])
                row_parts.append(jnp.concatenate([records[segment][3][8], own, exts[segment][1]], axis=1))
            grad_proj = jnp.concatenate(row_parts, axis=0).astype(jnp.bfloat16)
            grad_in_w = inner_rows(normed, grad_proj)
            grad_normed = outer_cols(grad_proj, in_weight[section_no])
            _, norm_back = jax.vjp(rms_scale, residual_in, pre_gain[section_no])
            grad_res, grad_pre = norm_back(grad_normed)
            cotangent = cotangent + grad_res
            grads[section_no] = (grad_pre, grad_in_w, small_acc[0], small_acc[1], small_acc[2], small_acc[3], small_acc[4], small_acc[5], grad_out_w)
        stacked = tuple((jnp.stack([grads[number][member] for number in range(LAYERS)]) for member in range(9)))
        new_totals = tuple((old + new for old, new in zip(totals, stacked)))
        return (new_totals, (block_out, cotangent))
    start_totals = tuple((jnp.zeros(weight.shape, jnp.float32) for weight in (pre_gain, in_weight, conv_weight, conv_bias, dt_bias, a_log, skip, norm_gain, out_weight)))
    series = (hidden_in.reshape(SEQS, SEQ_LEN, D), out_cot.reshape(SEQS, SEQ_LEN, D))
    totals, results = lax.scan(one_sequence, start_totals, series)
    return (results[0].reshape(ROWS, D), results[1].reshape(ROWS, D), totals[0], totals[1], totals[2], totals[3], totals[4], totals[5], totals[6], totals[7], totals[8])
```

```python
import jax
import jax.numpy as jnp
from jax import lax
from jax.experimental import pallas as pl
from jax.experimental.pallas import tpu as pltpu
from jax.sharding import PartitionSpec as P

DI = 1536
HEADS = 24
HEAD_DIM = 64
STATE = 128
CONV = 4
SPAN = 128
CHANNELS = DI + 2 * STATE
PAIR = 2 * HEAD_DIM
PAD = 8

EPS = 1e-05
EXACT = lax.Precision.HIGHEST
F32 = jnp.float32
BF16 = jnp.bfloat16


def swap(value, axis, bit):
    count = lax.axis_size(axis)
    return lax.ppermute(value, axis, [(i, i ^ bit) for i in range(count)])


def shift(value, axis, steps):
    count = lax.axis_size(axis)
    first, last = (max(0, -steps), min(count, count - steps))
    return lax.ppermute(value, axis, [(i, i + steps) for i in range(first, last)])


def bits_of(axis):
    bit, found = (1, [])
    while bit < lax.axis_size(axis):
        found.append(bit)
        bit *= 2
    return found


def gather_rows(own, after=None):
    if after is not None:
        own, _ = lax.optimization_barrier((own, after))
    rows = own.shape[0]
    me = lax.axis_index("shard")
    split = lax.axis_size("replica") > 1
    held = [(own, me * rows)]
    fetched = own
    for bit in reversed(bits_of("shard")):
        new = []
        for part, start in held:
            size = part.shape[0]
            there = start + (me ^ bit) * rows - me * rows
            if bit == 1 or not split or size % 32:
                new.append((swap(part, "shard", bit), there))
            else:
                half = size // 2
                low = (lax.axis_index("replica") & 1) * half
                mine = swap(lax.dynamic_slice_in_dim(part, low, half, 0), "shard", bit)
                new.append((mine, there + low))
                new.append((swap(mine, "replica", 1), there + half - low))
                fetched = mine
        held = held + new
    whole = jnp.zeros((rows * lax.axis_size("shard"), own.shape[1]), own.dtype)
    for part, start in held:
        whole = lax.dynamic_update_slice_in_dim(whole, part, start, 0)
    return whole, fetched


def weight_grad(left, right):
    count = lax.axis_size("shard")
    me = lax.axis_index("shard")
    place = lax.axis_index("replica")
    width = left.shape[1] // count

    def piece(k):
        columns = lax.dynamic_slice_in_dim(left, (me ^ k) * width, width, 1)
        return lax.dot_general(
            columns, right, (((0,), (0,)), ((), ())), preferred_element_type=F32
        )

    kept = {k: piece(k) for k in range(count)}
    for bit in bits_of("shard"):
        away = [k for k in kept if k & bit]
        got = {k ^ bit: swap(kept[k].astype(BF16), "shard", bit) for k in away}
        kept = {k: kept[k] + got[k].astype(F32) for k in got}
        kept = yield kept
    rows = kept[0]
    halved = []
    for bit in bits_of("replica"):
        if rows.shape[0] % 2:
            rows = rows + swap(rows.astype(BF16), "replica", bit).astype(F32)
        else:
            half = rows.shape[0] // 2
            mine = jnp.where((place & bit) != 0, half, 0)
            sent = lax.dynamic_slice_in_dim(rows, half - mine, half, 0).astype(BF16)
            rows = lax.dynamic_slice_in_dim(rows, mine, half, 0)
            rows = rows + swap(sent, "replica", bit).astype(F32)
            halved.append(bit)
        rows = yield rows
    rows = rows.astype(BF16)
    for bit in reversed(halved):
        other = swap(rows, "replica", bit)
        high = (place & bit) != 0
        rows = jnp.concatenate(
            [jnp.where(high, other, rows), jnp.where(high, rows, other)], axis=0
        )
        rows = yield rows
    return rows.astype(F32)


class Flow:
    def __init__(self, steps, points):
        self.steps, self.points = (steps, list(points))
        self.value, self.result = (next(steps), None)

    def advance(self):
        try:
            self.value = self.steps.send(self.value)
        except StopIteration as end:
            self.result = end.value

    def pass_point(self, point, array):
        while self.result is None and self.points and self.points[0] <= point:
            self.points.pop(0)
            self.value, array = lax.optimization_barrier((self.value, array))
            self.advance()
        return array

    def finish(self):
        while self.result is None:
            self.advance()
        return self.result


def sum_small(parts):
    flat = jnp.concatenate([part.reshape(-1) for part in parts])
    rows = -(-flat.size // (PAD * 128)) * PAD
    table = jnp.pad(flat, (0, rows * 128 - flat.size)).reshape(rows, 128)
    for axis in ("shard", "replica"):
        for bit in bits_of(axis):
            table = table + swap(table, axis, bit)
    flat, found, start = (table.reshape(-1), [], 0)
    for part in parts:
        found.append(flat[start : start + part.size].reshape(part.shape))
        start += part.size
    return found


def scan_states(decay, state, backward):
    me = lax.axis_index("shard")
    before, passed = (jnp.zeros_like(state), jnp.ones_like(decay))
    for bit in bits_of("shard"):
        other = swap(state.astype(BF16), "shard", bit).astype(F32)
        other_decay = swap(decay, "shard", bit)
        follows = (me & bit) == 0 if backward else (me & bit) != 0
        before = jnp.where(follows, before + passed * other, before)
        passed = jnp.where(follows, passed * other_decay, passed)
        state = jnp.where(follows, state + decay * other, other + other_decay * state)
        decay = decay * other_decay
    return before


def mm(left, right, dims=((1,), (0,)), exact=False):
    if exact:
        return lax.dot_general(
            left, right, (dims, ((), ())), precision=EXACT, preferred_element_type=F32
        )
    return lax.dot_general(
        left.astype(BF16), right.astype(BF16), (dims, ((), ())), preferred_element_type=F32
    )


COLS = ((1,), (1,))
ROWS = ((0,), (0,))


def iota(shape, axis):
    return lax.broadcasted_iota(jnp.int32, shape, axis)


def causal_mask(count):
    return iota((count, count), 0) >= iota((count, count), 1)


def low_lanes(count):
    return iota((count, PAIR), 1) < HEAD_DIM


def heads_of_channels():
    channel, head = (iota((DI, HEADS), 0), iota((DI, HEADS), 1))
    inside = (channel >= head * HEAD_DIM) & (channel < head * HEAD_DIM + HEAD_DIM)
    return jnp.where(inside, 1.0, 0.0).astype(F32)


def spread(values, h, low):
    return jnp.where(low, values[:, h : h + 1], values[:, h + 1 : h + 2])


def step_of(proj_ref, shift_ref):
    raw = proj_ref[:, DI + CHANNELS :].astype(F32) + shift_ref[...]
    return raw, jnp.maximum(raw, 0.0) + jnp.log1p(jnp.exp(-jnp.abs(raw)))


def sigmoid(v):
    return 1.0 / (1.0 + jnp.exp(-v))


def convolve(proj_ref, rim_ref, cw_ref, cb_ref, ext_ref):
    count = proj_ref.shape[0]
    ext_ref[0:PAD, :] = rim_ref[...].astype(F32)
    ext_ref[PAD : PAD + count, :] = proj_ref[:, DI : DI + CHANNELS].astype(F32)
    first = PAD - (CONV - 1)
    total = cb_ref[...] + cw_ref[0:1, :] * ext_ref[first : first + count, :]
    for k in range(1, CONV):
        total = total + cw_ref[k : k + 1, :] * ext_ref[first + k : first + k + count, :]
    return total


def forward_kernel(
    proj, rim, cw, cb, dtb, alog, skip, y_out, state_out, decay_out, act_out, log_out, ext
):
    count = proj.shape[0]
    conv = convolve(proj, rim, cw, cb, ext)
    act_out[...] = conv * sigmoid(conv)
    _, step = step_of(proj, dtb)
    rate = -step * jnp.exp(alog[...])
    causal = causal_mask(count)
    tril = jnp.where(causal, 1.0, 0.0).astype(F32)
    log = mm(tril, rate, exact=True)
    log_t = mm(rate, tril, ((0,), (1,)), exact=True)
    log_out[...] = log
    write = act_out[:, DI : DI + STATE]
    read = act_out[:, DI + STATE :]
    scores = jnp.where(causal, mm(read, write, COLS), 0.0)
    low = low_lanes(count)
    low_row = low_lanes(1)
    for h in range(0, HEADS, 2):
        lanes = slice(h * HEAD_DIM, h * HEAD_DIM + PAIR)
        x = act_out[:, lanes]
        logs = spread(log, h, low)
        weighted = x * spread(step, h, low)
        mixing = []
        for j in (h, h + 1):
            gap = jnp.where(causal, log[:, j : j + 1] - log_t[j : j + 1, :], -jnp.inf)
            mixing.append((jnp.exp(gap) * scores).astype(BF16))
        stacked = jnp.concatenate(
            [jnp.where(low, weighted, 0.0), jnp.where(low, 0.0, weighted)], axis=0
        )
        inside = mm(jnp.concatenate(mixing, axis=1), stacked)
        y_out[:, lanes] = inside + spread(skip, h, low_row) * x
        last = logs[count - 1 : count, :]
        state_out[:, lanes] = mm(write, weighted * jnp.exp(last - logs), ROWS)
        decay_out[:, lanes] = jnp.exp(last)


def gate_kernel(y_in, enter, act, log_ref, proj, gain, y_out, gated, scaled):
    count = proj.shape[0]
    log = log_ref[...]
    low = low_lanes(count)
    read = act[:, DI + STATE :]
    square = jnp.zeros((count, PAIR), F32)
    for h in range(0, HEADS, 2):
        lanes = slice(h * HEAD_DIM, h * HEAD_DIM + PAIR)
        y = y_in[:, lanes] + jnp.exp(spread(log, h, low)) * mm(read, enter[:, lanes])
        y_out[:, lanes] = y
        z = proj[:, lanes].astype(F32)
        t = y * (z * sigmoid(z))
        scaled[:, lanes] = t
        square = square + t * t
    scale = lax.rsqrt(jnp.sum(square, axis=1, keepdims=True) / DI + EPS)
    gated[...] = (scaled[...] * scale * gain[...]).astype(BF16)


def norm_back_kernel(
    grad, y, enter, act, log_ref, proj, gain, dy_out, dz_out, dgain_out, dstate_out, dread_out
):
    count = proj.shape[0]
    log = log_ref[...]
    low = low_lanes(count)
    read = act[:, DI + STATE :]
    square = jnp.zeros((count, PAIR), F32)
    along = jnp.zeros((count, PAIR), F32)
    for h in range(0, HEADS, 2):
        lanes = slice(h * HEAD_DIM, h * HEAD_DIM + PAIR)
        z = proj[:, lanes].astype(F32)
        t = y[:, lanes] * (z * sigmoid(z))
        square = square + t * t
        along = along + grad[:, lanes] * gain[:, lanes] * t
    scale = lax.rsqrt(jnp.sum(square, axis=1, keepdims=True) / DI + EPS)
    mean = jnp.sum(along, axis=1, keepdims=True) / DI * scale
    dread = jnp.zeros((count, STATE), F32)
    for h in range(0, HEADS, 2):
        lanes = slice(h * HEAD_DIM, h * HEAD_DIM + PAIR)
        z = proj[:, lanes].astype(F32)
        sig = sigmoid(z)
        gate = z * sig
        yy = y[:, lanes]
        unit = yy * gate * scale
        g = grad[:, lanes]
        dgain_out[:, lanes] = jnp.sum(g * unit, axis=0, keepdims=True)
        dt = scale * (g * gain[:, lanes] - unit * mean)
        dy = dt * gate
        dy_out[:, lanes] = dy
        dz_out[:, lanes] = (dt * yy * (sig * (1.0 + z * (1.0 - sig)))).astype(BF16)
        carried = (dy * jnp.exp(spread(log, h, low))).astype(BF16)
        dstate_out[:, lanes] = mm(read, carried, ROWS)
        dread = dread + mm(carried, enter[:, lanes], COLS)
    dread_out[...] = dread


def mix_back_kernel(
    dy_in, y, act, proj, dtb, alog, log_ref, skip, dread,
    dx_out, dwr_out, dstep_out, dlog_out, dskip_out, by_step, by_log
):
    count = proj.shape[0]
    _, step = step_of(proj, dtb)
    rate = -step * jnp.exp(alog[...])
    log = log_ref[...]
    causal = causal_mask(count)
    tril = jnp.where(causal, 1.0, 0.0).astype(F32)
    log_t = mm(rate, tril, ((0,), (1,)), exact=True)
    write = act[:, DI : DI + STATE]
    read = act[:, DI + STATE :]
    scores = mm(read, write, COLS)
    low = low_lanes(count)
    low_row = low_lanes(1)
    dscores = jnp.zeros((count, count), F32)
    onehot = heads_of_channels()
    dskip = jnp.zeros((1, HEADS), F32)
    for h in range(0, HEADS, 2):
        lanes = slice(h * HEAD_DIM, h * HEAD_DIM + PAIR)
        x = act[:, lanes]
        dy = dy_in[:, lanes]
        steps = spread(step, h, low)
        gain = spread(skip, h, low_row)
        decays = []
        for j in (h, h + 1):
            gap = jnp.where(causal, log[:, j : j + 1] - log_t[j : j + 1, :], -jnp.inf)
            decays.append(jnp.exp(gap))
        mixing = jnp.concatenate([(d * scores).astype(BF16) for d in decays], axis=0)
        dys = jnp.concatenate([jnp.where(low, dy, 0.0), jnp.where(low, 0.0, dy)], axis=0)
        dys = dys.astype(BF16)
        dweighted = mm(mixing, dys, ROWS)
        weighted = (x * steps).astype(BF16)
        dmix = mm(dys, weighted, COLS)
        dscores = dscores + decays[0] * dmix[:count] + decays[1] * dmix[count:]
        dx_out[:, lanes] = steps * dweighted + gain * dy
        by_step[:, lanes] = x * dweighted
        by_log[:, lanes] = (
            dy.astype(BF16).astype(F32) * (y[:, lanes] - gain * x)
            - weighted.astype(F32) * dweighted
        )
        dskip = dskip + mm(jnp.sum(dy * x, axis=0, keepdims=True), onehot[lanes, :], exact=True)
    dstep = mm(by_step[...], onehot, exact=True)
    dstep_out[...] = dstep
    dlog_out[...] = mm(by_log[...], onehot, exact=True)
    dskip_out[...] = dskip
    dwr_out[:, 0:STATE] = mm(dscores, read, ROWS)
    dwr_out[:, STATE:] = mm(dscores, write) + dread[...]


def finish_back_kernel(
    later, enter, act, proj, rim, cw, cb, dtb, alog, log_ref, dx_in, dwr, dstep_in, dlog_in,
    dxbc_out, drim_out, draw_out, dcw_out, dcb_out, ddtb_out, dalog_out, ext, dconv, by_step
):
    count = proj.shape[0]
    raw, step = step_of(proj, dtb)
    speed = -jnp.exp(alog[...])
    log = log_ref[...]
    low = low_lanes(count)
    onehot = heads_of_channels()
    conv = convolve(proj, rim, cw, cb, ext)
    sig = sigmoid(conv)
    dconv[0:PAD, :] = jnp.zeros((PAD, CHANNELS), F32)
    dconv[PAD + count :, :] = jnp.zeros((PAD, CHANNELS), F32)
    dconv[PAD : PAD + count, :] = sig * (1.0 + conv * (1.0 - sig))
    write = act[:, DI : DI + STATE].astype(BF16)
    dwrite = dwr[:, 0:STATE]
    for h in range(0, HEADS, 2):
        lanes = slice(h * HEAD_DIM, h * HEAD_DIM + PAIR)
        x = act[:, lanes]
        logs = spread(log, h, low)
        left = jnp.exp(logs[count - 1 : count, :] - logs)
        full = left * spread(step, h, low)
        into = mm(write, later[:, lanes])
        dx = dx_in[:, lanes] + full * into
        dconv[PAD : PAD + count, lanes] = dconv[PAD : PAD + count, lanes] * dx
        by_step[:, lanes] = x * left * into
        dwrite = dwrite + mm(x * full, later[:, lanes], COLS)
    rest = slice(PAD, PAD + count)
    dconv[rest, DI : DI + STATE] = dconv[rest, DI : DI + STATE] * dwrite
    dconv[rest, DI + STATE :] = dconv[rest, DI + STATE :] * dwr[:, STATE:]
    grown = mm(by_step[...], onehot, exact=True)
    dstep = dstep_in[...] + grown
    moved = step * grown
    held = mm(jnp.sum(later[...] * enter[...], axis=0, keepdims=True), onehot, exact=True)
    extra = jnp.sum(moved, axis=0, keepdims=True) + jnp.exp(log[count - 1 : count, :]) * held
    tril = jnp.where(causal_mask(count), 1.0, 0.0).astype(F32)
    drate = mm(tril, dlog_in[...] - moved, ROWS, exact=True) + extra
    dstep = dstep + drate * speed
    draw = dstep * sigmoid(raw)
    draw_out[...] = draw
    ddtb_out[...] = jnp.sum(draw, axis=0, keepdims=True)
    dalog_out[...] = jnp.sum(drate * step, axis=0, keepdims=True) * speed
    total = cw[0:1, :] * dconv[PAD + CONV - 1 : PAD + CONV - 1 + count, :]
    rims = cw[0:1, :] * dconv[CONV - 1 : CONV - 1 + PAD, :]
    first = PAD - (CONV - 1)
    for k in range(CONV):
        if k:
            off = CONV - 1 - k
            total = total + cw[k : k + 1, :] * dconv[PAD + off : PAD + off + count, :]
            rims = rims + cw[k : k + 1, :] * dconv[off : off + PAD, :]
        dcw_out[k : k + 1, :] = jnp.sum(
            dconv[rest, :] * ext[first + k : first + k + count, :], axis=0, keepdims=True
        )
    dxbc_out[...] = total
    drim_out[...] = rims
    dcb_out[...] = jnp.sum(dconv[rest, :], axis=0, keepdims=True)


def call(body, outs, scratch, *operands):
    return pl.pallas_call(
        body,
        out_shape=[jax.ShapeDtypeStruct(shape, kind) for shape, kind in outs],
        scratch_shapes=[pltpu.VMEM(shape, F32) for shape in scratch],
    )(*operands)


def rms_scale(residual, gain):
    mean_sq = jnp.mean(residual * residual, axis=-1, keepdims=True)
    return residual * lax.rsqrt(mean_sq + EPS) * gain


def outer_cols(left, right):
    return lax.dot_general(left, right, (((1,), (1,)), ((), ())), preferred_element_type=F32)


def shards(
    hidden_in,
    out_cot,
    pre_gain,
    in_weight,
    conv_weight,
    conv_bias,
    dt_bias,
    a_log,
    skip,
    norm_gain,
    out_weight,
):
    layer_count = in_weight.shape[0]
    rim_width = CONV - 1
    residual = hidden_in.astype(F32)
    count = residual.shape[0]
    assert count == SPAN
    wide, heads = ((count, DI), (count, HEADS))
    ext_shape = (count + PAD, CHANNELS)
    whole_in, whole_out, fetched = ([], [], None)
    for n in range(layer_count):
        for weight, wholes in ((in_weight, whole_in), (out_weight, whole_out)):
            whole, fetched = gather_rows(weight[n], fetched)
            wholes.append(whole)
    saved = []
    for n in range(layer_count):
        normed = rms_scale(residual, pre_gain[n]).astype(BF16)
        projected = jnp.dot(normed, whole_in[n], preferred_element_type=F32).astype(BF16)
        rim_rows = shift(projected[count - rim_width :, DI : DI + CHANNELS], "shard", 1)
        rim = jnp.pad(rim_rows, ((PAD - rim_width, 0), (0, 0)))
        params = (dt_bias[n][None], a_log[n][None])
        taps = (conv_weight[n], conv_bias[n][None])
        y_part, state, decay, act, log = call(
            forward_kernel,
            [(wide, F32), ((STATE, DI), F32), ((1, DI), F32), ((count, CHANNELS), F32),
             (heads, F32)],
            [ext_shape],
            projected, rim, *taps, *params, skip[n][None],
        )
        enter = scan_states(decay, state, False)
        y, gated = call(
            gate_kernel, [(wide, F32), (wide, BF16)], [wide],
            y_part, enter, act, log, projected, norm_gain[n][None],
        )
        mixed = jnp.dot(gated, whole_out[n], preferred_element_type=F32)
        saved.append((residual, normed, projected, rim, enter, gated, act, log, y, decay))
        residual = residual + mixed
    block_out = residual.astype(BF16)
    cotangent = out_cot.astype(F32)
    big_in = [None] * layer_count
    big_out = [None] * layer_count
    small = [None] * layer_count
    flows, point = ([], 0)

    def pass_points(array):
        nonlocal point
        for flow in flows:
            array = flow.pass_point(point, array)
        point += 1
        return array

    for n in reversed(range(layer_count)):
        residual_in, normed, projected, rim, enter, gated, act, log, y, decay = saved[n]
        params = (dt_bias[n][None], a_log[n][None])
        taps = (conv_weight[n], conv_bias[n][None])
        cot_b = cotangent.astype(BF16)
        big_out[n] = Flow(weight_grad(gated, cot_b), [point + k for k in (1, 3, 4, 6, 7, 8, 9, 10)])
        flows.append(big_out[n])
        grad_gated = pass_points(outer_cols(cot_b, whole_out[n]))
        dy, dz, dgain, dstate, dread = call(
            norm_back_kernel,
            [(wide, F32), (wide, BF16), ((1, DI), F32), ((STATE, DI), F32),
             ((count, STATE), F32)],
            [],
            grad_gated, y, enter, act, log, projected, norm_gain[n][None],
        )
        dy = pass_points(dy)
        later = pass_points(scan_states(decay, dstate, True))
        dx, dwr, dstep, dlog, dskip = call(
            mix_back_kernel,
            [(wide, F32), ((count, 2 * STATE), F32), (heads, F32), (heads, F32),
             ((1, HEADS), F32)],
            [wide, wide],
            dy, y, act, projected, *params, log, skip[n][None], dread,
        )
        dx = pass_points(dx)
        dxbc, drim, draw, dcw, dcb, ddtb, dalog = call(
            finish_back_kernel,
            [((count, CHANNELS), F32), ((PAD, CHANNELS), F32), (heads, F32),
             ((CONV, CHANNELS), F32), ((1, CHANNELS), F32), ((1, HEADS), F32),
             ((1, HEADS), F32)],
            [ext_shape, (count + 2 * PAD, CHANNELS), wide],
            later, enter, act, projected, rim, *taps, *params, log, dx, dwr, dstep, dlog,
        )
        dxbc = pass_points(dxbc)
        returned = shift(drim[PAD - rim_width :], "shard", -1)
        dxbc = dxbc + jnp.pad(returned, ((count - rim_width, 0), (0, 0)))
        grad_proj = jnp.concatenate([dz, dxbc.astype(BF16), draw.astype(BF16)], axis=1)
        big_in[n] = Flow(weight_grad(normed, grad_proj), [point + 1 + k for k in (0, 3, 4)])
        flows.append(big_in[n])
        grad_normed = pass_points(outer_cols(grad_proj, whole_in[n]))
        _, norm_back = jax.vjp(rms_scale, residual_in, pre_gain[n])
        grad_res, grad_pre = norm_back(grad_normed)
        cotangent = cotangent + grad_res
        small[n] = sum_small((grad_pre, dcw, dcb[0], ddtb[0], dalog[0], dskip[0], dgain[0]))
    for turn in reversed(range(layer_count)):
        big_out[turn] = big_out[turn].finish()
        big_in[turn] = big_in[turn].finish()
    summed = [jnp.stack([small[n][member] for n in range(layer_count)]) for member in range(7)]
    return (
        block_out,
        cotangent,
        summed[0],
        jnp.stack(big_in),
        summed[1],
        summed[2],
        summed[3],
        summed[4],
        summed[5],
        summed[6],
        jnp.stack(big_out),
    )


def solution(mesh):
    return jax.shard_map(
        shards,
        mesh=mesh,
        in_specs=(
            P(("replica", "shard"), None),
            P(("replica", "shard"), None),
            P(),
            P(None, "shard", None),
            P(),
            P(),
            P(),
            P(),
            P(),
            P(),
            P(None, "shard", None),
        ),
        out_specs=(
            P(("replica", "shard"), None),
            P(("replica", "shard"), None),
            P(),
            P(None, "shard", None),
            P(),
            P(),
            P(),
            P(),
            P(),
            P(),
            P(None, "shard", None),
        ),
        check_vma=False,
    )
```

```python
import jax
import jax.numpy as jnp
from jax import lax
from jax.experimental import pallas as pl
from jax.experimental.pallas import tpu as pltpu
from jax.sharding import PartitionSpec as P

DI = 1536
HEADS = 24
HEAD_DIM = 64
STATE = 128
CONV = 4
SPAN = 128
CHANNELS = DI + 2 * STATE
PAIR = 2 * HEAD_DIM
PAD = 8

EPS = 1e-05
EXACT = lax.Precision.HIGHEST
F32 = jnp.float32
BF16 = jnp.bfloat16


def swap(value, axis, bit):
    count = lax.axis_size(axis)
    return lax.ppermute(value, axis, [(i, i ^ bit) for i in range(count)])


def shift(value, axis, steps):
    count = lax.axis_size(axis)
    first, last = (max(0, -steps), min(count, count - steps))
    return lax.ppermute(value, axis, [(i, i + steps) for i in range(first, last)])


def bits_of(axis):
    bit, found = (1, [])
    while bit < lax.axis_size(axis):
        found.append(bit)
        bit *= 2
    return found


def gather_rows(own, after=None):
    if after is not None:
        own, _ = lax.optimization_barrier((own, after))
    rows = own.shape[0]
    me = lax.axis_index("shard")
    split = lax.axis_size("replica") > 1
    held = [(own, me * rows)]
    fetched = own
    for bit in reversed(bits_of("shard")):
        new = []
        for part, start in held:
            size = part.shape[0]
            there = start + (me ^ bit) * rows - me * rows
            if bit == 1 or not split or size % 32:
                new.append((swap(part, "shard", bit), there))
            else:
                half = size // 2
                low = (lax.axis_index("replica") & 1) * half
                mine = swap(lax.dynamic_slice_in_dim(part, low, half, 0), "shard", bit)
                new.append((mine, there + low))
                new.append((swap(mine, "replica", 1), there + half - low))
                fetched = mine
        held = held + new
    whole = jnp.zeros((rows * lax.axis_size("shard"), own.shape[1]), own.dtype)
    for part, start in held:
        whole = lax.dynamic_update_slice_in_dim(whole, part, start, 0)
    return whole, fetched


def weight_grad(left, right):
    count = lax.axis_size("shard")
    me = lax.axis_index("shard")
    place = lax.axis_index("replica")
    width = left.shape[1] // count

    def piece(k):
        columns = lax.dynamic_slice_in_dim(left, (me ^ k) * width, width, 1)
        return lax.dot_general(
            columns, right, (((0,), (0,)), ((), ())), preferred_element_type=F32
        )

    kept = {k: piece(k) for k in range(count)}
    for bit in bits_of("shard"):
        away = [k for k in kept if k & bit]
        got = {k ^ bit: swap(kept[k].astype(BF16), "shard", bit) for k in away}
        kept = {k: kept[k] + got[k].astype(F32) for k in got}
        kept = yield kept
    rows = kept[0]
    halved = []
    for bit in bits_of("replica"):
        if rows.shape[0] % 2:
            rows = rows + swap(rows.astype(BF16), "replica", bit).astype(F32)
        else:
            half = rows.shape[0] // 2
            mine = jnp.where((place & bit) != 0, half, 0)
            sent = lax.dynamic_slice_in_dim(rows, half - mine, half, 0).astype(BF16)
            rows = lax.dynamic_slice_in_dim(rows, mine, half, 0)
            rows = rows + swap(sent, "replica", bit).astype(F32)
            halved.append(bit)
        rows = yield rows
    rows = rows.astype(BF16)
    for bit in reversed(halved):
        other = swap(rows, "replica", bit)
        high = (place & bit) != 0
        rows = jnp.concatenate(
            [jnp.where(high, other, rows), jnp.where(high, rows, other)], axis=0
        )
        rows = yield rows
    return rows.astype(F32)


class Flow:
    def __init__(self, steps, points):
        self.steps, self.points = (steps, list(points))
        self.value, self.result = (next(steps), None)

    def advance(self):
        try:
            self.value = self.steps.send(self.value)
        except StopIteration as end:
            self.result = end.value

    def pass_point(self, point, array):
        while self.result is None and self.points and self.points[0] <= point:
            self.points.pop(0)
            self.value, array = lax.optimization_barrier((self.value, array))
            self.advance()
        return array

    def finish(self):
        while self.result is None:
            self.advance()
        return self.result


def sum_small(parts):
    flat = jnp.concatenate([part.reshape(-1) for part in parts])
    rows = -(-flat.size // (PAD * 128)) * PAD
    table = jnp.pad(flat, (0, rows * 128 - flat.size)).reshape(rows, 128)
    for axis in ("shard", "replica"):
        for bit in bits_of(axis):
            table = table + swap(table, axis, bit)
    flat, found, start = (table.reshape(-1), [], 0)
    for part in parts:
        found.append(flat[start : start + part.size].reshape(part.shape))
        start += part.size
    return found


def scan_states(decay, state, backward):
    me = lax.axis_index("shard")
    before, passed = (jnp.zeros_like(state), jnp.ones_like(decay))
    for bit in bits_of("shard"):
        other = swap(state.astype(BF16), "shard", bit).astype(F32)
        other_decay = swap(decay, "shard", bit)
        follows = (me & bit) == 0 if backward else (me & bit) != 0
        before = jnp.where(follows, before + passed * other, before)
        passed = jnp.where(follows, passed * other_decay, passed)
        state = jnp.where(follows, state + decay * other, other + other_decay * state)
        decay = decay * other_decay
    return before


def mm(left, right, dims=((1,), (0,)), exact=False):
    if exact:
        return lax.dot_general(
            left, right, (dims, ((), ())), precision=EXACT, preferred_element_type=F32
        )
    return lax.dot_general(
        left.astype(BF16), right.astype(BF16), (dims, ((), ())), preferred_element_type=F32
    )


COLS = ((1,), (1,))
ROWS = ((0,), (0,))


def iota(shape, axis):
    return lax.broadcasted_iota(jnp.int32, shape, axis)


def causal_mask(count):
    return iota((count, count), 0) >= iota((count, count), 1)


def low_lanes(count):
    return iota((count, PAIR), 1) < HEAD_DIM


def heads_of_channels():
    channel, head = (iota((DI, HEADS), 0), iota((DI, HEADS), 1))
    inside = (channel >= head * HEAD_DIM) & (channel < head * HEAD_DIM + HEAD_DIM)
    return jnp.where(inside, 1.0, 0.0).astype(F32)


def spread(values, h, low):
    return jnp.where(low, values[:, h : h + 1], values[:, h + 1 : h + 2])


def step_of(proj_ref, shift_ref):
    raw = proj_ref[:, DI + CHANNELS :].astype(F32) + shift_ref[...]
    return raw, jnp.maximum(raw, 0.0) + jnp.log1p(jnp.exp(-jnp.abs(raw)))


def sigmoid(v):
    return 1.0 / (1.0 + jnp.exp(-v))


def convolve(proj_ref, rim_ref, cw_ref, cb_ref, ext_ref):
    count = proj_ref.shape[0]
    ext_ref[0:PAD, :] = rim_ref[...].astype(F32)
    ext_ref[PAD : PAD + count, :] = proj_ref[:, DI : DI + CHANNELS].astype(F32)
    first = PAD - (CONV - 1)
    total = cb_ref[...] + cw_ref[0:1, :] * ext_ref[first : first + count, :]
    for k in range(1, CONV):
        total = total + cw_ref[k : k + 1, :] * ext_ref[first + k : first + k + count, :]
    return total


def forward_kernel(
    proj, rim, cw, cb, dtb, alog, skip, y_out, state_out, decay_out, act_out, log_out, ext
):
    count = proj.shape[0]
    conv = convolve(proj, rim, cw, cb, ext)
    act_out[...] = conv * sigmoid(conv)
    _, step = step_of(proj, dtb)
    rate = -step * jnp.exp(alog[...])
    causal = causal_mask(count)
    tril = jnp.where(causal, 1.0, 0.0).astype(F32)
    log = mm(tril, rate, exact=True)
    log_t = mm(rate, tril, ((0,), (1,)), exact=True)
    log_out[...] = log
    write = act_out[:, DI : DI + STATE]
    read = act_out[:, DI + STATE :]
    scores = jnp.where(causal, mm(read, write, COLS), 0.0)
    low = low_lanes(count)
    low_row = low_lanes(1)
    for h in range(0, HEADS, 2):
        lanes = slice(h * HEAD_DIM, h * HEAD_DIM + PAIR)
        x = act_out[:, lanes]
        logs = spread(log, h, low)
        weighted = x * spread(step, h, low)
        mixing = []
        for j in (h, h + 1):
            gap = jnp.where(causal, log[:, j : j + 1] - log_t[j : j + 1, :], -jnp.inf)
            mixing.append((jnp.exp(gap) * scores).astype(BF16))
        stacked = jnp.concatenate(
            [jnp.where(low, weighted, 0.0), jnp.where(low, 0.0, weighted)], axis=0
        )
        inside = mm(jnp.concatenate(mixing, axis=1), stacked)
        y_out[:, lanes] = inside + spread(skip, h, low_row) * x
        last = logs[count - 1 : count, :]
        state_out[:, lanes] = mm(write, weighted * jnp.exp(last - logs), ROWS)
        decay_out[:, lanes] = jnp.exp(last)


def gate_kernel(y_in, enter, act, log_ref, proj, gain, y_out, gated, scaled):
    count = proj.shape[0]
    log = log_ref[...]
    low = low_lanes(count)
    read = act[:, DI + STATE :]
    square = jnp.zeros((count, PAIR), F32)
    for h in range(0, HEADS, 2):
        lanes = slice(h * HEAD_DIM, h * HEAD_DIM + PAIR)
        y = y_in[:, lanes] + jnp.exp(spread(log, h, low)) * mm(read, enter[:, lanes])
        y_out[:, lanes] = y
        z = proj[:, lanes].astype(F32)
        t = y * (z * sigmoid(z))
        scaled[:, lanes] = t
        square = square + t * t
    scale = lax.rsqrt(jnp.sum(square, axis=1, keepdims=True) / DI + EPS)
    gated[...] = (scaled[...] * scale * gain[...]).astype(BF16)


def norm_back_kernel(
    grad, y, enter, act, log_ref, proj, gain, dy_out, dz_out, dgain_out, dstate_out, dread_out
):
    count = proj.shape[0]
    log = log_ref[...]
    low = low_lanes(count)
    read = act[:, DI + STATE :]
    square = jnp.zeros((count, PAIR), F32)
    along = jnp.zeros((count, PAIR), F32)
    for h in range(0, HEADS, 2):
        lanes = slice(h * HEAD_DIM, h * HEAD_DIM + PAIR)
        z = proj[:, lanes].astype(F32)
        t = y[:, lanes] * (z * sigmoid(z))
        square = square + t * t
        along = along + grad[:, lanes] * gain[:, lanes] * t
    scale = lax.rsqrt(jnp.sum(square, axis=1, keepdims=True) / DI + EPS)
    mean = jnp.sum(along, axis=1, keepdims=True) / DI * scale
    dread = jnp.zeros((count, STATE), F32)
    for h in range(0, HEADS, 2):
        lanes = slice(h * HEAD_DIM, h * HEAD_DIM + PAIR)
        z = proj[:, lanes].astype(F32)
        sig = sigmoid(z)
        gate = z * sig
        yy = y[:, lanes]
        unit = yy * gate * scale
        g = grad[:, lanes]
        dgain_out[:, lanes] = jnp.sum(g * unit, axis=0, keepdims=True)
        dt = scale * (g * gain[:, lanes] - unit * mean)
        dy = dt * gate
        dy_out[:, lanes] = dy
        dz_out[:, lanes] = (dt * yy * (sig * (1.0 + z * (1.0 - sig)))).astype(BF16)
        carried = (dy * jnp.exp(spread(log, h, low))).astype(BF16)
        dstate_out[:, lanes] = mm(read, carried, ROWS)
        dread = dread + mm(carried, enter[:, lanes], COLS)
    dread_out[...] = dread


def mix_back_kernel(
    dy_in, y, act, proj, dtb, alog, log_ref, skip, dread,
    dx_out, dwr_out, dstep_out, dlog_out, dskip_out, by_step, by_log
):
    count = proj.shape[0]
    _, step = step_of(proj, dtb)
    rate = -step * jnp.exp(alog[...])
    log = log_ref[...]
    causal = causal_mask(count)
    tril = jnp.where(causal, 1.0, 0.0).astype(F32)
    log_t = mm(rate, tril, ((0,), (1,)), exact=True)
    write = act[:, DI : DI + STATE]
    read = act[:, DI + STATE :]
    scores = mm(read, write, COLS)
    low = low_lanes(count)
    low_row = low_lanes(1)
    dscores = jnp.zeros((count, count), F32)
    onehot = heads_of_channels()
    dskip = jnp.zeros((1, HEADS), F32)
    for h in range(0, HEADS, 2):
        lanes = slice(h * HEAD_DIM, h * HEAD_DIM + PAIR)
        x = act[:, lanes]
        dy = dy_in[:, lanes]
        steps = spread(step, h, low)
        gain = spread(skip, h, low_row)
        decays = []
        for j in (h, h + 1):
            gap = jnp.where(causal, log[:, j : j + 1] - log_t[j : j + 1, :], -jnp.inf)
            decays.append(jnp.exp(gap))
        mixing = jnp.concatenate([(d * scores).astype(BF16) for d in decays], axis=0)
        dys = jnp.concatenate([jnp.where(low, dy, 0.0), jnp.where(low, 0.0, dy)], axis=0)
        dys = dys.astype(BF16)
        dweighted = mm(mixing, dys, ROWS)
        weighted = (x * steps).astype(BF16)
        dmix = mm(dys, weighted, COLS)
        dscores = dscores + decays[0] * dmix[:count] + decays[1] * dmix[count:]
        dx_out[:, lanes] = steps * dweighted + gain * dy
        by_step[:, lanes] = x * dweighted
        by_log[:, lanes] = (
            dy.astype(BF16).astype(F32) * (y[:, lanes] - gain * x)
            - weighted.astype(F32) * dweighted
        )
        dskip = dskip + mm(jnp.sum(dy * x, axis=0, keepdims=True), onehot[lanes, :], exact=True)
    dstep = mm(by_step[...], onehot, exact=True)
    dstep_out[...] = dstep
    dlog_out[...] = mm(by_log[...], onehot, exact=True)
    dskip_out[...] = dskip
    dwr_out[:, 0:STATE] = mm(dscores, read, ROWS)
    dwr_out[:, STATE:] = mm(dscores, write) + dread[...]


def finish_back_kernel(
    later, enter, act, proj, rim, cw, cb, dtb, alog, log_ref, dx_in, dwr, dstep_in, dlog_in,
    dxbc_out, drim_out, draw_out, dcw_out, dcb_out, ddtb_out, dalog_out, ext, dconv, by_step
):
    count = proj.shape[0]
    raw, step = step_of(proj, dtb)
    speed = -jnp.exp(alog[...])
    log = log_ref[...]
    low = low_lanes(count)
    onehot = heads_of_channels()
    conv = convolve(proj, rim, cw, cb, ext)
    sig = sigmoid(conv)
    dconv[0:PAD, :] = jnp.zeros((PAD, CHANNELS), F32)
    dconv[PAD + count :, :] = jnp.zeros((PAD, CHANNELS), F32)
    dconv[PAD : PAD + count, :] = sig * (1.0 + conv * (1.0 - sig))
    write = act[:, DI : DI + STATE].astype(BF16)
    dwrite = dwr[:, 0:STATE]
    for h in range(0, HEADS, 2):
        lanes = slice(h * HEAD_DIM, h * HEAD_DIM + PAIR)
        x = act[:, lanes]
        logs = spread(log, h, low)
        left = jnp.exp(logs[count - 1 : count, :] - logs)
        full = left * spread(step, h, low)
        into = mm(write, later[:, lanes])
        dx = dx_in[:, lanes] + full * into
        dconv[PAD : PAD + count, lanes] = dconv[PAD : PAD + count, lanes] * dx
        by_step[:, lanes] = x * left * into
        dwrite = dwrite + mm(x * full, later[:, lanes], COLS)
    rest = slice(PAD, PAD + count)
    dconv[rest, DI : DI + STATE] = dconv[rest, DI : DI + STATE] * dwrite
    dconv[rest, DI + STATE :] = dconv[rest, DI + STATE :] * dwr[:, STATE:]
    grown = mm(by_step[...], onehot, exact=True)
    dstep = dstep_in[...] + grown
    moved = step * grown
    held = mm(jnp.sum(later[...] * enter[...], axis=0, keepdims=True), onehot, exact=True)
    extra = jnp.sum(moved, axis=0, keepdims=True) + jnp.exp(log[count - 1 : count, :]) * held
    tril = jnp.where(causal_mask(count), 1.0, 0.0).astype(F32)
    drate = mm(tril, dlog_in[...] - moved, ROWS, exact=True) + extra
    dstep = dstep + drate * speed
    draw = dstep * sigmoid(raw)
    draw_out[...] = draw
    ddtb_out[...] = jnp.sum(draw, axis=0, keepdims=True)
    dalog_out[...] = jnp.sum(drate * step, axis=0, keepdims=True) * speed
    total = cw[0:1, :] * dconv[PAD + CONV - 1 : PAD + CONV - 1 + count, :]
    rims = cw[0:1, :] * dconv[CONV - 1 : CONV - 1 + PAD, :]
    first = PAD - (CONV - 1)
    for k in range(CONV):
        if k:
            off = CONV - 1 - k
            total = total + cw[k : k + 1, :] * dconv[PAD + off : PAD + off + count, :]
            rims = rims + cw[k : k + 1, :] * dconv[off : off + PAD, :]
        dcw_out[k : k + 1, :] = jnp.sum(
            dconv[rest, :] * ext[first + k : first + k + count, :], axis=0, keepdims=True
        )
    dxbc_out[...] = total
    drim_out[...] = rims
    dcb_out[...] = jnp.sum(dconv[rest, :], axis=0, keepdims=True)


def call(body, outs, scratch, *operands):
    return pl.pallas_call(
        body,
        out_shape=[jax.ShapeDtypeStruct(shape, kind) for shape, kind in outs],
        scratch_shapes=[pltpu.VMEM(shape, F32) for shape in scratch],
    )(*operands)


def rms_scale(residual, gain):
    mean_sq = jnp.mean(residual * residual, axis=-1, keepdims=True)
    return residual * lax.rsqrt(mean_sq + EPS) * gain


def outer_cols(left, right):
    return lax.dot_general(left, right, (((1,), (1,)), ((), ())), preferred_element_type=F32)


def shards(
    hidden_in,
    out_cot,
    pre_gain,
    in_weight,
    conv_weight,
    conv_bias,
    dt_bias,
    a_log,
    skip,
    norm_gain,
    out_weight,
):
    layer_count = in_weight.shape[0]
    rim_width = CONV - 1
    residual = hidden_in.astype(F32)
    count = residual.shape[0]
    assert count == SPAN
    wide, heads = ((count, DI), (count, HEADS))
    ext_shape = (count + PAD, CHANNELS)
    whole_in, whole_out, fetched = ([], [], None)
    for n in range(layer_count):
        for weight, wholes in ((in_weight, whole_in), (out_weight, whole_out)):
            whole, fetched = gather_rows(weight[n], fetched)
            wholes.append(whole)
    saved = []
    for n in range(layer_count):
        normed = rms_scale(residual, pre_gain[n]).astype(BF16)
        projected = jnp.dot(normed, whole_in[n], preferred_element_type=F32).astype(BF16)
        rim_rows = shift(projected[count - rim_width :, DI : DI + CHANNELS], "shard", 1)
        rim = jnp.pad(rim_rows, ((PAD - rim_width, 0), (0, 0)))
        params = (dt_bias[n][None], a_log[n][None])
        taps = (conv_weight[n], conv_bias[n][None])
        y_part, state, decay, act, log = call(
            forward_kernel,
            [(wide, F32), ((STATE, DI), F32), ((1, DI), F32), ((count, CHANNELS), F32),
             (heads, F32)],
            [ext_shape],
            projected, rim, *taps, *params, skip[n][None],
        )
        enter = scan_states(decay, state, False)
        y, gated = call(
            gate_kernel, [(wide, F32), (wide, BF16)], [wide],
            y_part, enter, act, log, projected, norm_gain[n][None],
        )
        mixed = jnp.dot(gated, whole_out[n], preferred_element_type=F32)
        saved.append((residual, normed, projected, rim, enter, gated, act, log, y, decay))
        residual = residual + mixed
    block_out = residual.astype(BF16)
    cotangent = out_cot.astype(F32)
    big_in = [None] * layer_count
    big_out = [None] * layer_count
    small = [None] * layer_count
    flows, point = ([], 0)

    def pass_points(array):
        nonlocal point
        for flow in flows:
            array = flow.pass_point(point, array)
        point += 1
        return array

    for n in reversed(range(layer_count)):
        residual_in, normed, projected, rim, enter, gated, act, log, y, decay = saved[n]
        params = (dt_bias[n][None], a_log[n][None])
        taps = (conv_weight[n], conv_bias[n][None])
        cot_b = cotangent.astype(BF16)
        big_out[n] = Flow(weight_grad(gated, cot_b), [point + k for k in (1, 3, 4, 6, 7, 8, 9, 10)])
        flows.append(big_out[n])
        grad_gated = pass_points(outer_cols(cot_b, whole_out[n]))
        dy, dz, dgain, dstate, dread = call(
            norm_back_kernel,
            [(wide, F32), (wide, BF16), ((1, DI), F32), ((STATE, DI), F32),
             ((count, STATE), F32)],
            [],
            grad_gated, y, enter, act, log, projected, norm_gain[n][None],
        )
        gate_flow = Flow(weight_grad(normed, dz), [point + k for k in (2, 4, 6, 7, 8, 9)])
        flows.append(gate_flow)
        dy = pass_points(dy)
        later = pass_points(scan_states(decay, dstate, True))
        dx, dwr, dstep, dlog, dskip = call(
            mix_back_kernel,
            [(wide, F32), ((count, 2 * STATE), F32), (heads, F32), (heads, F32),
             ((1, HEADS), F32)],
            [wide, wide],
            dy, y, act, projected, *params, log, skip[n][None], dread,
        )
        dx = pass_points(dx)
        dxbc, drim, draw, dcw, dcb, ddtb, dalog = call(
            finish_back_kernel,
            [((count, CHANNELS), F32), ((PAD, CHANNELS), F32), (heads, F32),
             ((CONV, CHANNELS), F32), ((1, CHANNELS), F32), ((1, HEADS), F32),
             ((1, HEADS), F32)],
            [ext_shape, (count + 2 * PAD, CHANNELS), wide],
            later, enter, act, projected, rim, *taps, *params, log, dx, dwr, dstep, dlog,
        )
        dxbc = pass_points(dxbc)
        returned = shift(drim[PAD - rim_width :], "shard", -1)
        dxbc = dxbc + jnp.pad(returned, ((count - rim_width, 0), (0, 0)))
        grad_proj = jnp.concatenate([dz, dxbc.astype(BF16), draw.astype(BF16)], axis=1)
        rest_flow = Flow(
            weight_grad(normed, grad_proj[:, DI:]), [point + k for k in (1, 4, 5)]
        )
        flows.append(rest_flow)
        big_in[n] = (gate_flow, rest_flow)
        grad_normed = pass_points(outer_cols(grad_proj, whole_in[n]))
        _, norm_back = jax.vjp(rms_scale, residual_in, pre_gain[n])
        grad_res, grad_pre = norm_back(grad_normed)
        cotangent = cotangent + grad_res
        small[n] = sum_small((grad_pre, dcw, dcb[0], ddtb[0], dalog[0], dskip[0], dgain[0]))
    for turn in reversed(range(layer_count)):
        big_out[turn] = big_out[turn].finish()
        big_in[turn] = jnp.concatenate([flow.finish() for flow in big_in[turn]], axis=1)
    summed = [jnp.stack([small[n][member] for n in range(layer_count)]) for member in range(7)]
    return (
        block_out,
        cotangent,
        summed[0],
        jnp.stack(big_in),
        summed[1],
        summed[2],
        summed[3],
        summed[4],
        summed[5],
        summed[6],
        jnp.stack(big_out),
    )


def solution(mesh):
    return jax.shard_map(
        shards,
        mesh=mesh,
        in_specs=(
            P(("replica", "shard"), None),
            P(("replica", "shard"), None),
            P(),
            P(None, "shard", None),
            P(),
            P(),
            P(),
            P(),
            P(),
            P(),
            P(None, "shard", None),
        ),
        out_specs=(
            P(("replica", "shard"), None),
            P(("replica", "shard"), None),
            P(),
            P(None, "shard", None),
            P(),
            P(),
            P(),
            P(),
            P(),
            P(),
            P(None, "shard", None),
        ),
        check_vma=False,
    )
```
